256 devices in a mesh: op: 32 (over y, x, z_lo), sec: 8 (over z_hi, core).
Axes of the slice: x: 4, y: 4, z: 8 (z_hi: 4, z_lo: 2; z = z_hi * 2 + z_lo), core: 2. Of those that a mesh axis runs over, the one named last changes fastest.
Arguments:
- psi: bfloat16 [16, 256, 256], P('sec', 'op'), may hold values from -6 to 6
- left_ops: bfloat16 [12288, 256, 256], P(('op', 'sec')), may hold values from -0.375 to 0.375
- right_ops: bfloat16 [12288, 256, 256], P(('op', 'sec')), may hold values from -0.013671875 to 0.013671875
- in_sector: int32 [12288], P(('op', 'sec')), may hold values from 0 to 15
- out_sector: int32 [12288], P(('op', 'sec')), may hold values from 0 to 15
- live_terms: int32 [256], P(('op', 'sec')), may hold values from 1 to 48, as said below
Outputs:
- sigma: float32 [16, 256, 256], P('sec', 'op')
The draws below stay inside these ranges and needn't reach their ends.
Inputs may be any that keep to these rules, and one draw needn't show every extreme that they name: live_terms[d] counts the leading slots of device d (numbered as in the reference program: op index * number of sec indices + sec index) that are used; slots beyond it are ignored; some device is full in every draw.
All inputs are finite; a program needn't handle non-finite values.
Results may differ from the reference program's by a relative error of at most 0.0029.
Values may be sent and summed in bfloat16 or wider, within the bound.
No kernel may reach another device: no remote copies, remote signals or barrier semaphores. Data moves between devices by JAX's collectives and lax.ppermute only.
A program may use at most 64 MiB of HBM per device.

```python
import jax
import jax.numpy as jnp
from jax import lax

B = 256
SEC_DEV = 2
TB_DEV = 48
NSEC = 16
RANKS = 256
TERMS = 12288
N_OP = 32


def draw_live_terms(key, part):
    first, second = jax.random.split(key)
    shifts = jax.random.randint(first, (RANKS,), 0, 4)
    full_rank = jax.random.randint(second, (), 0, RANKS)
    shifts = jnp.where(jnp.arange(RANKS) == full_rank, 0, shifts)
    counts = TB_DEV // jnp.left_shift(jnp.int32(1), shifts)
    return jnp.maximum(counts, 1).astype(jnp.int32)


def place_ends(drawn, rng, low, top_value):
    extent = drawn.shape
    spot = [jax.random.randint(jax.random.fold_in(rng, axis), (), 0, extent[axis]) for axis in range(len(extent))]
    drawn = drawn.at[tuple(spot)].set(low)
    longest = extent.index(max(extent))
    spot[longest] = (spot[longest] + 1) % extent[longest]
    return drawn.at[tuple(spot)].set(top_value)


def shard_levels(key, shape, cuts, low, high):
    def one(dim, shards_of):
        draws = jax.random.uniform(jax.random.fold_in(jax.random.fold_in(key, 6), dim), (shards_of,), jnp.float32, low / len(cuts), high / len(cuts))
        return jnp.repeat(jnp.exp(draws), shape[dim] // shards_of).reshape((-1,) + (1,) * (len(shape) - dim - 1))

    loudness = one(*cuts[0])
    for cut in cuts[1:]:
        loudness = loudness * one(*cut)
    return loudness


def gaussian(rng, shape, deviation, most, cuts=(), kind=jnp.bfloat16):
    result = jax.random.normal(rng, shape, jnp.float32) * deviation
    if len(cuts) > 0:
        result = shard_levels(rng, shape, cuts, -0.22, 0.18) * result
    return jnp.clip(result, min=-most, max=most).astype(kind)


def setup_inputs(seed: int = 0) -> dict:
    splits = jax.random.split(jax.random.key(seed), 7)
    return {
        "psi": gaussian(splits[0], (NSEC, B, B), 1.0, 6.0, ((0, 8), (1, 32))),
        "left_ops": gaussian(splits[1], (TERMS, B, B), B ** -0.5, 0.375, ((0, 256),)),
        "right_ops": gaussian(splits[2], (TERMS, B, B), (B * TB_DEV * N_OP // SEC_DEV) ** -0.5, 0.013671875, ((0, 256),)),
        "in_sector": place_ends(jax.random.randint(splits[3], (TERMS,), 0, NSEC), jax.random.fold_in(splits[3], 1), 0, NSEC - 1).astype(jnp.int32),
        "out_sector": place_ends(jax.random.randint(splits[4], (TERMS,), 0, NSEC), jax.random.fold_in(splits[4], 1), 0, NSEC - 1).astype(jnp.int32),
        "live_terms": draw_live_terms(jax.random.fold_in(splits[6], 71), 0),
    }


def reference(psi, left_ops, right_ops, in_sector, out_sector, live_terms):
    slots = jnp.arange(TERMS, dtype=jnp.int32)
    owner = slots // TB_DEV
    used = ((slots % TB_DEV) < live_terms[owner]).astype(jnp.float32)
    group = 64
    count = TERMS // group if TERMS % group == 0 else TERMS // 4
    size = TERMS // count
    lefts = left_ops.reshape(count, size, B, B)
    rights = right_ops.reshape(count, size, B, B)
    ins = in_sector.reshape(count, size)
    outs = out_sector.reshape(count, size)
    masks = used.reshape(count, size)
    sectors = jnp.arange(NSEC, dtype=jnp.int32)

    def step(total, pieces):
        left, right, ids_in, ids_out, mask = pieces
        blocks = jnp.take(psi, ids_in, axis=0).astype(jnp.float32)
        middle = jnp.einsum("tij,tjk->tik", left.astype(jnp.float32), blocks).astype(jnp.bfloat16)
        contribution = jnp.einsum("tik,tlk->til", middle.astype(jnp.float32), right.astype(jnp.float32))
        onehot = (ids_out[:, None] == sectors[None, :]).astype(jnp.float32) * mask[:, None]
        total = total + jnp.einsum("ts,til->sil", onehot, contribution, precision=lax.Precision.HIGHEST)
        return total, None

    start = jnp.zeros((NSEC, B, B), jnp.float32)
    sigma, _ = lax.scan(step, start, (lefts, rights, ins, outs, masks))
    return sigma
```

```python
import jax
import jax.numpy as jnp
from jax import lax
from jax.experimental import pallas as pl
from jax.experimental.pallas import tpu as pltpu
from jax.sharding import Mesh, PartitionSpec as P

AXES = ("y", "x", "zl", "zh", "c")
SIZES = (4, 4, 2, 4, 2)
STEP = 4


def swap_cores(value):
    return lax.ppermute(value, "c", [(0, 1), (1, 0)])


def spread(value, axes, count):
    copies = jnp.broadcast_to(value[None], (count,) + value.shape)
    return lax.all_to_all(copies, axes, 0, 0)


def product_kernel(ids_in, ids_out, scalars, mine, theirs, left, right, keep, send, psi, total, sems):
    step = pl.program_id(0)
    live = scalars[0]
    core = scalars[1]

    def copies():
        for side in range(2):
            source = mine if side == 0 else theirs
            owner = core if side == 0 else 1 - core
            for high in range(4):
                for low in range(2):
                    sector = 4 * high + 2 * owner + low
                    yield pltpu.make_async_copy(
                        source.at[:, high, low], psi.at[sector], sems.at[side * 8 + high * 2 + low]
                    )

    @pl.when(step == 0)
    def _():
        for copy in copies():
            copy.start()
        total[...] = jnp.zeros_like(total)
        for copy in copies():
            copy.wait()

    for offset in range(STEP):
        term = step * STEP + offset

        @pl.when(term < live)
        def _():
            block = psi[ids_in[term]].reshape(256, 256)
            middle = jnp.dot(left[offset], block, preferred_element_type=jnp.float32)
            product = lax.dot_general(
                middle.astype(jnp.bfloat16),
                right[offset],
                (((1,), (1,)), ((), ())),
                preferred_element_type=jnp.float32,
            )
            out = ids_out[term]
            total[out] = total[out] + product

    @pl.when(step == pl.num_programs(0) - 1)
    def _():
        for high in range(4):
            for low in range(2):
                keep[high * 2 + low] = total[4 * high + 2 * core + low]
                send[high * 2 + low] = total[4 * high + 2 * (1 - core) + low].astype(jnp.bfloat16)


def product(ids_in, ids_out, scalars, mine, theirs, left, right):
    terms = left.shape[0]

    def term_block(step, ids_in, ids_out, scalars):
        return (jnp.minimum(step, (scalars[0] - 1) // STEP), 0, 0)

    return pl.pallas_call(
        product_kernel,
        grid_spec=pltpu.PrefetchScalarGridSpec(
            num_scalar_prefetch=3,
            grid=(terms // STEP,),
            in_specs=[
                pl.BlockSpec(memory_space=pl.ANY),
                pl.BlockSpec(memory_space=pl.ANY),
                pl.BlockSpec((STEP, 256, 256), term_block),
                pl.BlockSpec((STEP, 256, 256), term_block),
            ],
            out_specs=[
                pl.BlockSpec((8, 256, 256), lambda step, *_: (0, 0, 0)),
                pl.BlockSpec((8, 256, 256), lambda step, *_: (0, 0, 0)),
            ],
            scratch_shapes=[
                pltpu.VMEM((16, 32, 8, 256), jnp.bfloat16),
                pltpu.VMEM((16, 256, 256), jnp.float32),
                pltpu.SemaphoreType.DMA((16,)),
            ],
        ),
        out_shape=[
            jax.ShapeDtypeStruct((8, 256, 256), jnp.float32),
            jax.ShapeDtypeStruct((8, 256, 256), jnp.bfloat16),
        ],
        compiler_params=pltpu.CompilerParams(vmem_limit_bytes=32 * 2**20),
    )(ids_in, ids_out, scalars, mine, theirs, left, right)


def merge_kernel(keep, other, out):
    for group in range(out.shape[0]):
        rows = pl.ds(group * 16, 16)
        out[group] = (keep[:, rows, :] + other[:, rows, :].astype(jnp.float32)).astype(jnp.bfloat16)


def merge(keep, other):
    return pl.pallas_call(
        merge_kernel,
        grid=(4,),
        in_specs=[pl.BlockSpec((8, 64, 256), lambda step: (0, step, 0))] * 2,
        out_specs=pl.BlockSpec((4, 8, 16, 256), lambda step: (step, 0, 0, 0)),
        out_shape=jax.ShapeDtypeStruct((16, 8, 16, 256), jnp.bfloat16),
    )(keep, other)


def local(psi, left_ops, right_ops, in_sector, out_sector, live_terms):
    by_z = spread(psi, "zh", 4)
    mine = spread(by_z, ("y", "x", "zl"), 32)
    theirs = swap_cores(mine)
    scalars = jnp.stack([live_terms[0], lax.axis_index("c").astype(jnp.int32)])
    keep, send = product(in_sector, out_sector, scalars, mine, theirs, left_ops, right_ops)
    other = swap_cores(send)
    blocks = merge(keep, other)
    arrived = lax.all_to_all(blocks, ("y", "x"), 0, 0)
    rows = arrived.astype(jnp.float32).sum(0)
    pieces = rows.reshape(4, 2, 2, 8, 256).transpose(0, 2, 1, 3, 4).reshape(8, 2, 8, 256)
    last = lax.all_to_all(pieces, ("zh", "zl"), 0, 0)
    return last.sum(0)


def solution(mesh):
    torus = Mesh(mesh.devices.reshape(SIZES), AXES)
    op = ("y", "x", "zl")
    sec = ("zh", "c")
    return jax.shard_map(
        local,
        mesh=torus,
        in_specs=(
            P(sec, op, None),
            P(op + sec, None, None),
            P(op + sec, None, None),
            P(op + sec),
            P(op + sec),
            P(op + sec),
        ),
        out_specs=P(sec, op, None),
        check_vma=False,
    )
```

```python
import jax
import jax.numpy as jnp
from jax import lax
from jax.experimental import pallas as pl
from jax.experimental.pallas import tpu as pltpu
from jax.sharding import Mesh, PartitionSpec as P

AXES = ("y", "x", "zl", "zh", "c")
SIZES = (4, 4, 2, 4, 2)
STEP = 8
GROUP = 4
UNUSED = 16


def swap_cores(value):
    return lax.ppermute(value, "c", [(0, 1), (1, 0)])


def spread(value, axes, count):
    copies = jnp.broadcast_to(value[None], (count,) + value.shape)
    return lax.all_to_all(copies, axes, 0, 0)


def product_kernel(table, mine, theirs, left, right, total, send, psi, lefts, rights, psi_sems, sems):
    live = table[0]
    core = table[1]
    terms = left.shape[0]
    chunks = terms // STEP

    gathered = [
        pltpu.make_async_copy(mine, psi.at[core], psi_sems.at[0]),
        pltpu.make_async_copy(theirs, psi.at[1 - core], psi_sems.at[1]),
    ]

    def loads(chunk):
        part = pl.ds(chunk * STEP, STEP)
        return [
            pltpu.make_async_copy(left.at[part], lefts.at[part], sems.at[0, chunk]),
            pltpu.make_async_copy(right.at[part], rights.at[part], sems.at[1, chunk]),
        ]

    for copy in gathered:
        copy.start()
    for chunk in range(chunks):
        for copy in loads(chunk):
            copy.start()
    total[...] = jnp.zeros_like(total)
    for copy in gathered:
        copy.wait()

    def run(chunk, carry):
        for copy in loads(chunk):
            copy.wait()
        for first in range(0, STEP, GROUP):
            middles = []
            for offset in range(first, first + GROUP):
                term = chunk * STEP + offset
                sector = table[2 + term]
                block = psi[(sector >> 1) & 1, :, sector >> 2, sector & 1].reshape(256, 256)
                middle = jnp.dot(lefts[term], block, preferred_element_type=jnp.float32)
                middles.append(middle.astype(jnp.bfloat16))
            for offset in range(first, first + GROUP):
                term = chunk * STEP + offset
                out = jnp.where(term < live, table[2 + terms + term], UNUSED)
                total[out] = total[out] + lax.dot_general(
                    middles[offset - first],
                    rights[term],
                    (((1,), (1,)), ((), ())),
                    preferred_element_type=jnp.float32,
                )
        return carry

    def drain(chunk, carry):
        for copy in loads(chunk):
            copy.wait()
        return carry

    used = lax.div(live + STEP - 1, STEP)
    lax.fori_loop(0, used, run, 0)
    lax.fori_loop(used, chunks, drain, 0)
    for high in range(4):
        for low in range(2):
            send[high * 2 + low] = total[4 * high + 2 * (1 - core) + low].astype(jnp.bfloat16)


def product(table, mine, theirs, left, right):
    terms = left.shape[0]
    smem = pl.BlockSpec(memory_space=pltpu.SMEM)
    vmem = pl.BlockSpec(memory_space=pltpu.VMEM)
    hbm = pl.BlockSpec(memory_space=pltpu.HBM)
    anywhere = pl.BlockSpec(memory_space=pl.ANY)
    return pl.pallas_call(
        product_kernel,
        in_specs=[smem, anywhere, anywhere, hbm, hbm],
        out_specs=[vmem, vmem],
        scratch_shapes=[
            pltpu.VMEM((2, 32, 4, 2, 8, 256), jnp.bfloat16),
            pltpu.VMEM((terms, 256, 256), jnp.bfloat16),
            pltpu.VMEM((terms, 256, 256), jnp.bfloat16),
            pltpu.SemaphoreType.DMA((2,)),
            pltpu.SemaphoreType.DMA((2, terms // STEP)),
        ],
        out_shape=[
            jax.ShapeDtypeStruct((UNUSED + 1, 256, 256), jnp.float32),
            jax.ShapeDtypeStruct((8, 256, 256), jnp.bfloat16),
        ],
        compiler_params=pltpu.CompilerParams(vmem_limit_bytes=44 * 2**20),
    )(table, mine, theirs, left, right)


def merge_kernel(table, total, other, out):
    core = table[1]
    for pair in range(8):
        sector = 4 * (pair // 2) + 2 * core + pair % 2
        for group in range(16):
            rows = pl.ds(group * 16, 16)
            summed = total[sector, rows, :] + other[pair, rows, :].astype(jnp.float32)
            out[group, pair] = summed.astype(jnp.bfloat16)


def merge(table, total, other):
    vmem = pl.BlockSpec(memory_space=pltpu.VMEM)
    return pl.pallas_call(
        merge_kernel,
        in_specs=[pl.BlockSpec(memory_space=pltpu.SMEM), vmem, vmem],
        out_specs=vmem,
        out_shape=jax.ShapeDtypeStruct((16, 8, 16, 256), jnp.bfloat16),
        compiler_params=pltpu.CompilerParams(vmem_limit_bytes=16 * 2**20),
    )(table, total, other)


def local(psi, left_ops, right_ops, in_sector, out_sector, live_terms):
    by_z = spread(psi, "zh", 4)
    mine = spread(by_z, ("y", "x", "zl"), 32)
    theirs = swap_cores(mine)
    core = lax.axis_index("c").astype(jnp.int32)
    table = jnp.concatenate([live_terms, core[None], in_sector, out_sector])
    total, send = product(table, mine, theirs, left_ops, right_ops)
    other = swap_cores(send)
    blocks = merge(table, total, other)
    arrived = lax.all_to_all(blocks, ("y", "x"), 0, 0)
    rows = arrived.astype(jnp.float32).sum(0)
    pieces = rows.reshape(4, 2, 2, 8, 256).transpose(0, 2, 1, 3, 4).reshape(8, 2, 8, 256)
    last = lax.all_to_all(pieces, ("zh", "zl"), 0, 0)
    return last.sum(0)


def solution(mesh):
    torus = Mesh(mesh.devices.reshape(SIZES), AXES)
    op = ("y", "x", "zl")
    sec = ("zh", "c")
    return jax.shard_map(
        local,
        mesh=torus,
        in_specs=(
            P(sec, op, None),
            P(op + sec, None, None),
            P(op + sec, None, None),
            P(op + sec),
            P(op + sec),
            P(op + sec),
        ),
        out_specs=P(sec, op, None),
        check_vma=False,
    )
```

```python
import jax
import jax.numpy as jnp
from jax import lax
from jax.experimental import pallas as pl
from jax.experimental.pallas import tpu as pltpu
from jax.sharding import Mesh, PartitionSpec as P

AXES = ("y", "x", "zl", "zh", "c")
SIZES = (4, 4, 2, 4, 2)
EARLY = 8
CHUNK = 4
LOAD_MIB = 48
PRODUCT_MIB = 40
STEP = 8
GROUP = 4
UNUSED = 16


ANY = pl.BlockSpec(memory_space=pl.ANY)
HBM = pl.BlockSpec(memory_space=pltpu.HBM)
SMEM = pl.BlockSpec(memory_space=pltpu.SMEM)
VMEM = pl.BlockSpec(memory_space=pltpu.VMEM)


def swap_cores(value):
    return lax.ppermute(value, "c", [(0, 1), (1, 0)])


def spread(value, axes, count):
    copies = jnp.broadcast_to(value[None], (count,) + value.shape)
    return lax.all_to_all(copies, axes, 0, 0)


def load_kernel(left, right, lefts, rights, sems):
    copies = []
    for chunk in range(lefts.shape[0] // CHUNK):
        part = pl.ds(chunk * CHUNK, CHUNK)
        copies.append(pltpu.make_async_copy(left.at[part], lefts.at[part], sems.at[0, chunk]))
        copies.append(pltpu.make_async_copy(right.at[part], rights.at[part], sems.at[1, chunk]))
    for copy in copies:
        copy.start()
    for copy in copies:
        copy.wait()


def load(left, right):
    part = jax.ShapeDtypeStruct((EARLY,) + left.shape[1:], left.dtype)
    return pl.pallas_call(
        load_kernel,
        in_specs=[HBM, HBM],
        out_specs=[VMEM, VMEM],
        out_shape=[part, part],
        scratch_shapes=[pltpu.SemaphoreType.DMA((2, EARLY // CHUNK))],
        cost_estimate=pl.CostEstimate(flops=0, transcendentals=0, bytes_accessed=EARLY * 2**18),
        compiler_params=pltpu.CompilerParams(vmem_limit_bytes=LOAD_MIB * 2**20),
    )(left, right)


def product_kernel(
    in_sector, out_sector, live_terms, mine, theirs, early_left, early_right, left, right,
    total, send, psi, lefts, rights, ins, outs, lives, psi_sems, id_sems, sems,
):
    terms = left.shape[0]
    core = lax.axis_index("c")
    gathered = [
        pltpu.make_async_copy(mine, psi.at[core], psi_sems.at[0]),
        pltpu.make_async_copy(theirs, psi.at[1 - core], psi_sems.at[1]),
    ]
    numbers = [
        pltpu.make_async_copy(in_sector, ins, id_sems.at[0]),
        pltpu.make_async_copy(out_sector, outs, id_sems.at[1]),
        pltpu.make_async_copy(live_terms, lives, id_sems.at[2]),
    ]

    def loads(chunk):
        source = pl.ds(EARLY + chunk * CHUNK, CHUNK)
        part = pl.ds(chunk * CHUNK, CHUNK)
        return [
            pltpu.make_async_copy(left.at[source], lefts.at[part], sems.at[0, chunk]),
            pltpu.make_async_copy(right.at[source], rights.at[part], sems.at[1, chunk]),
        ]

    def wait(chunk, carry):
        for copy in loads(chunk):
            copy.wait()
        return carry

    chunks = (terms - EARLY) // CHUNK
    for copy in numbers:
        copy.start()
    for chunk in range(chunks):
        for copy in loads(chunk):
            copy.start()
    for copy in gathered:
        copy.start()
    total[...] = jnp.zeros_like(total)
    for copy in gathered:
        copy.wait()
    for copy in numbers:
        copy.wait()
    live = lives[0]

    def add(first, shift, lefts, rights):
        for low in range(0, STEP, GROUP):
            middles = []
            for offset in range(low, low + GROUP):
                term = first + offset
                sector = ins[term]
                block = psi[(sector >> 1) & 1, :, sector >> 2, sector & 1].reshape(256, 256)
                middle = jnp.dot(lefts[term - shift], block, preferred_element_type=jnp.float32)
                middles.append(middle.astype(jnp.bfloat16))
            for offset in range(low, low + GROUP):
                term = first + offset
                out = jnp.where(term < live, outs[term], UNUSED)
                total[out] = total[out] + lax.dot_general(
                    middles[offset - low],
                    rights[term - shift],
                    (((1,), (1,)), ((), ())),
                    preferred_element_type=jnp.float32,
                )

    def early_step(step, carry):
        add(step * STEP, 0, early_left, early_right)
        return carry

    def late_step(step, carry):
        lax.fori_loop(step * (STEP // CHUNK), (step + 1) * (STEP // CHUNK), wait, 0)
        add(EARLY + step * STEP, EARLY, lefts, rights)
        return carry

    used = lax.div(live + STEP - 1, STEP)
    lax.fori_loop(0, jnp.minimum(used, EARLY // STEP), early_step, 0)
    late = jnp.maximum(used - EARLY // STEP, 0)
    lax.fori_loop(0, late, late_step, 0)
    lax.fori_loop(late * (STEP // CHUNK), chunks, wait, 0)
    for high in range(4):
        for low in range(2):
            send[high * 2 + low] = total[4 * high + 2 * (1 - core) + low].astype(jnp.bfloat16)


def product(in_sector, out_sector, live_terms, mine, theirs, early_left, early_right, left, right):
    terms = left.shape[0]
    return pl.pallas_call(
        product_kernel,
        in_specs=[HBM] * 3 + [ANY, ANY, VMEM, VMEM, HBM, HBM],
        out_specs=[VMEM, VMEM],
        scratch_shapes=[
            pltpu.VMEM((2, 32, 4, 2, 8, 256), jnp.bfloat16),
            pltpu.VMEM((terms - EARLY, 256, 256), jnp.bfloat16),
            pltpu.VMEM((terms - EARLY, 256, 256), jnp.bfloat16),
            pltpu.SMEM(in_sector.shape, in_sector.dtype),
            pltpu.SMEM(out_sector.shape, out_sector.dtype),
            pltpu.SMEM(live_terms.shape, live_terms.dtype),
            pltpu.SemaphoreType.DMA((2,)),
            pltpu.SemaphoreType.DMA((3,)),
            pltpu.SemaphoreType.DMA((2, (terms - EARLY) // CHUNK)),
        ],
        out_shape=[
            jax.ShapeDtypeStruct((UNUSED + 1, 256, 256), jnp.float32),
            jax.ShapeDtypeStruct((8, 256, 256), jnp.bfloat16),
        ],
        cost_estimate=pl.CostEstimate(flops=terms * 2**26, transcendentals=0, bytes_accessed=terms * 2**18),
        compiler_params=pltpu.CompilerParams(vmem_limit_bytes=PRODUCT_MIB * 2**20),
    )(in_sector, out_sector, live_terms, mine, theirs, early_left, early_right, left, right)


def merge_kernel(total, other, out):
    core = lax.axis_index("c")
    for pair in range(8):
        sector = 4 * (pair // 2) + 2 * core + pair % 2
        for group in range(16):
            rows = pl.ds(group * 16, 16)
            summed = total[sector, rows, :] + other[pair, rows, :].astype(jnp.float32)
            out[group, pair] = summed.astype(jnp.bfloat16)


def merge(total, other):
    return pl.pallas_call(
        merge_kernel,
        in_specs=[VMEM, VMEM],
        out_specs=VMEM,
        out_shape=jax.ShapeDtypeStruct((16, 8, 16, 256), jnp.bfloat16),
        compiler_params=pltpu.CompilerParams(vmem_limit_bytes=6 * 2**20),
    )(total, other)


def local(psi, left_ops, right_ops, in_sector, out_sector, live_terms):
    by_z = spread(psi, "zh", 4)
    mine = spread(by_z, ("y", "x", "zl"), 32)
    theirs = swap_cores(mine)
    early_left, early_right = load(left_ops, right_ops)
    total, send = product(
        in_sector, out_sector, live_terms, mine, theirs, early_left, early_right, left_ops, right_ops
    )
    other = swap_cores(send)
    blocks = merge(total, other)
    arrived = lax.all_to_all(blocks, ("y", "x"), 0, 0)
    rows = arrived.astype(jnp.float32).sum(0)
    pieces = rows.reshape(4, 2, 2, 8, 256).transpose(0, 2, 1, 3, 4).reshape(8, 2, 8, 256)
    last = lax.all_to_all(pieces, ("zh", "zl"), 0, 0)
    return last.sum(0)


def solution(mesh):
    torus = Mesh(mesh.devices.reshape(SIZES), AXES)
    op = ("y", "x", "zl")
    sec = ("zh", "c")
    return jax.shard_map(
        local,
        mesh=torus,
        in_specs=(
            P(sec, op, None),
            P(op + sec, None, None),
            P(op + sec, None, None),
            P(op + sec),
            P(op + sec),
            P(op + sec),
        ),
        out_specs=P(sec, op, None),
        check_vma=False,
    )
```

```python
import jax
import jax.numpy as jnp
from jax import lax
from jax.experimental import pallas as pl
from jax.experimental.pallas import tpu as pltpu
from jax.sharding import Mesh, PartitionSpec as P

AXES = ("y", "x", "zl", "zh", "c")
SIZES = (4, 4, 2, 4, 2)
EARLY = 8
CHUNK = 4
LOAD_MIB = 48
PRODUCT_MIB = 40
STEP = 8
GROUP = 4
UNUSED = 16


ANY = pl.BlockSpec(memory_space=pl.ANY)
HBM = pl.BlockSpec(memory_space=pltpu.HBM)
SMEM = pl.BlockSpec(memory_space=pltpu.SMEM)
VMEM = pl.BlockSpec(memory_space=pltpu.VMEM)


def swap_cores(value):
    return lax.ppermute(value, "c", [(0, 1), (1, 0)])


def spread(value, axes, count):
    copies = jnp.broadcast_to(value[None], (count,) + value.shape)
    return lax.all_to_all(copies, axes, 0, 0)


def load_kernel(left, right, lefts, rights, sems):
    copies = []
    for chunk in range(lefts.shape[0] // CHUNK):
        part = pl.ds(chunk * CHUNK, CHUNK)
        copies.append(pltpu.make_async_copy(left.at[part], lefts.at[part], sems.at[0, chunk]))
        copies.append(pltpu.make_async_copy(right.at[part], rights.at[part], sems.at[1, chunk]))
    for copy in copies:
        copy.start()
    for copy in copies:
        copy.wait()


def load(left, right):
    part = jax.ShapeDtypeStruct((EARLY,) + left.shape[1:], left.dtype)
    return pl.pallas_call(
        load_kernel,
        in_specs=[HBM, HBM],
        out_specs=[VMEM, VMEM],
        out_shape=[part, part],
        scratch_shapes=[pltpu.SemaphoreType.DMA((2, EARLY // CHUNK))],
        cost_estimate=pl.CostEstimate(flops=0, transcendentals=0, bytes_accessed=EARLY * 2**18),
        compiler_params=pltpu.CompilerParams(vmem_limit_bytes=LOAD_MIB * 2**20),
    )(left, right)


def product_kernel(
    in_sector, out_sector, live_terms, mine, theirs, early_left, early_right, left, right,
    total, send, psi, lefts, rights, ins, outs, lives, psi_sems, id_sems, sems,
):
    terms = left.shape[0]
    core = lax.axis_index("c")
    gathered = [
        pltpu.make_async_copy(mine, psi.at[core], psi_sems.at[0]),
        pltpu.make_async_copy(theirs, psi.at[1 - core], psi_sems.at[1]),
    ]
    numbers = [
        pltpu.make_async_copy(in_sector, ins, id_sems.at[0]),
        pltpu.make_async_copy(out_sector, outs, id_sems.at[1]),
        pltpu.make_async_copy(live_terms, lives, id_sems.at[2]),
    ]

    def loads(chunk):
        source = pl.ds(EARLY + chunk * CHUNK, CHUNK)
        part = pl.ds(chunk * CHUNK, CHUNK)
        return [
            pltpu.make_async_copy(left.at[source], lefts.at[part], sems.at[0, chunk]),
            pltpu.make_async_copy(right.at[source], rights.at[part], sems.at[1, chunk]),
        ]

    def wait(chunk, carry):
        for copy in loads(chunk):
            copy.wait()
        return carry

    chunks = (terms - EARLY) // CHUNK
    for copy in numbers:
        copy.start()
    for chunk in range(chunks):
        for copy in loads(chunk):
            copy.start()
    for copy in gathered:
        copy.start()
    total[...] = jnp.zeros_like(total)
    for copy in gathered:
        copy.wait()
    for copy in numbers:
        copy.wait()
    live = lives[0]

    def add(first, shift, lefts, rights):
        for low in range(0, STEP, GROUP):
            middles = []
            for offset in range(low, low + GROUP):
                term = first + offset
                sector = ins[term]
                high = pl.ds((sector >> 2) * 2, 2)
                block = psi[(sector >> 1) & 1, :, high, sector & 1].reshape(256, 256)
                middle = jnp.dot(lefts[term - shift], block, preferred_element_type=jnp.float32)
                middles.append(middle.astype(jnp.bfloat16))
            for offset in range(low, low + GROUP):
                term = first + offset
                out = jnp.where(term < live, outs[term], UNUSED)
                total[out] = total[out] + lax.dot_general(
                    middles[offset - low],
                    rights[term - shift],
                    (((1,), (1,)), ((), ())),
                    preferred_element_type=jnp.float32,
                )

    def early_step(step, carry):
        add(step * STEP, 0, early_left, early_right)
        return carry

    def late_step(step, carry):
        lax.fori_loop(step * (STEP // CHUNK), (step + 1) * (STEP // CHUNK), wait, 0)
        add(EARLY + step * STEP, EARLY, lefts, rights)
        return carry

    used = lax.div(live + STEP - 1, STEP)
    lax.fori_loop(0, jnp.minimum(used, EARLY // STEP), early_step, 0)
    late = jnp.maximum(used - EARLY // STEP, 0)
    lax.fori_loop(0, late, late_step, 0)
    lax.fori_loop(late * (STEP // CHUNK), chunks, wait, 0)
    for high in range(4):
        for low in range(2):
            send[high * 2 + low] = total[4 * high + 2 * (1 - core) + low].astype(jnp.bfloat16)


def product(in_sector, out_sector, live_terms, mine, theirs, early_left, early_right, left, right):
    terms = left.shape[0]
    return pl.pallas_call(
        product_kernel,
        in_specs=[HBM] * 3 + [ANY, ANY, VMEM, VMEM, HBM, HBM],
        out_specs=[VMEM, VMEM],
        scratch_shapes=[
            pltpu.VMEM((2, 16, 8, 2, 8, 256), jnp.bfloat16),
            pltpu.VMEM((terms - EARLY, 256, 256), jnp.bfloat16),
            pltpu.VMEM((terms - EARLY, 256, 256), jnp.bfloat16),
            pltpu.SMEM(in_sector.shape, in_sector.dtype),
            pltpu.SMEM(out_sector.shape, out_sector.dtype),
            pltpu.SMEM(live_terms.shape, live_terms.dtype),
            pltpu.SemaphoreType.DMA((2,)),
            pltpu.SemaphoreType.DMA((3,)),
            pltpu.SemaphoreType.DMA((2, (terms - EARLY) // CHUNK)),
        ],
        out_shape=[
            jax.ShapeDtypeStruct((UNUSED + 1, 256, 256), jnp.float32),
            jax.ShapeDtypeStruct((8, 256, 256), jnp.bfloat16),
        ],
        cost_estimate=pl.CostEstimate(flops=terms * 2**26, transcendentals=0, bytes_accessed=terms * 2**18),
        compiler_params=pltpu.CompilerParams(vmem_limit_bytes=PRODUCT_MIB * 2**20),
    )(in_sector, out_sector, live_terms, mine, theirs, early_left, early_right, left, right)


def merge_kernel(total, other, out):
    core = lax.axis_index("c")
    for pair in range(8):
        sector = 4 * (pair // 2) + 2 * core + pair % 2
        for group in range(16):
            rows = pl.ds(group * 16, 16)
            summed = total[sector, rows, :] + other[pair, rows, :].astype(jnp.float32)
            out[group, pair] = summed.astype(jnp.bfloat16)


def merge(total, other):
    return pl.pallas_call(
        merge_kernel,
        in_specs=[VMEM, VMEM],
        out_specs=VMEM,
        out_shape=jax.ShapeDtypeStruct((16, 8, 16, 256), jnp.bfloat16),
        compiler_params=pltpu.CompilerParams(vmem_limit_bytes=6 * 2**20),
    )(total, other)


def local(psi, left_ops, right_ops, in_sector, out_sector, live_terms):
    by_z = spread(psi, ("zh", "zl"), 8)
    mine = spread(by_z, ("y", "x"), 16)
    theirs = swap_cores(mine)
    early_left, early_right = load(left_ops, right_ops)
    total, send = product(
        in_sector, out_sector, live_terms, mine, theirs, early_left, early_right, left_ops, right_ops
    )
    other = swap_cores(send)
    blocks = merge(total, other)
    arrived = lax.all_to_all(blocks, ("y", "x"), 0, 0)
    rows = arrived.astype(jnp.float32).sum(0)
    pieces = rows.reshape(4, 2, 2, 8, 256).transpose(0, 2, 1, 3, 4).reshape(8, 2, 8, 256)
    last = lax.all_to_all(pieces, ("zh", "zl"), 0, 0)
    return last.sum(0)


def solution(mesh):
    torus = Mesh(mesh.devices.reshape(SIZES), AXES)
    op = ("y", "x", "zl")
    sec = ("zh", "c")
    return jax.shard_map(
        local,
        mesh=torus,
        in_specs=(
            P(sec, op, None),
            P(op + sec, None, None),
            P(op + sec, None, None),
            P(op + sec),
            P(op + sec),
            P(op + sec),
        ),
        out_specs=P(sec, op, None),
        check_vma=False,
    )
```

```python
import jax
import jax.numpy as jnp
from jax import lax
from jax.experimental import pallas as pl
from jax.experimental.pallas import tpu as pltpu
from jax.sharding import Mesh, PartitionSpec as P

AXES = ("y", "x", "zl", "zh", "c")
SIZES = (4, 4, 2, 4, 2)
EARLY = 8
CHUNK = 4
LOAD_MIB = 48
PRODUCT_MIB = 40
STEP = 8
GROUP = 4
UNUSED = 16


ANY = pl.BlockSpec(memory_space=pl.ANY)
HBM = pl.BlockSpec(memory_space=pltpu.HBM)
SMEM = pl.BlockSpec(memory_space=pltpu.SMEM)
VMEM = pl.BlockSpec(memory_space=pltpu.VMEM)


def swap_cores(value):
    return lax.ppermute(value, "c", [(0, 1), (1, 0)])


def spread(value, axes, count):
    copies = jnp.broadcast_to(value[None], (count,) + value.shape)
    return lax.all_to_all(copies, axes, 0, 0)


def load_kernel(left, right, lefts, rights, sems):
    copies = []
    for chunk in range(lefts.shape[0] // CHUNK):
        part = pl.ds(chunk * CHUNK, CHUNK)
        copies.append(pltpu.make_async_copy(left.at[part], lefts.at[part], sems.at[0, chunk]))
        copies.append(pltpu.make_async_copy(right.at[part], rights.at[part], sems.at[1, chunk]))
    for copy in copies:
        copy.start()
    for copy in copies:
        copy.wait()


def load(left, right):
    part = jax.ShapeDtypeStruct((EARLY,) + left.shape[1:], left.dtype)
    return pl.pallas_call(
        load_kernel,
        in_specs=[HBM, HBM],
        out_specs=[VMEM, VMEM],
        out_shape=[part, part],
        scratch_shapes=[pltpu.SemaphoreType.DMA((2, EARLY // CHUNK))],
        cost_estimate=pl.CostEstimate(flops=0, transcendentals=0, bytes_accessed=EARLY * 2**18),
        compiler_params=pltpu.CompilerParams(vmem_limit_bytes=LOAD_MIB * 2**20),
    )(left, right)


def product_kernel(
    in_sector, out_sector, live_terms, mine, theirs, early_left, early_right, left, right,
    total, send, psi, lefts, rights, ins, outs, lives, psi_sems, id_sems, sems,
):
    terms = left.shape[0]
    core = lax.axis_index("c")
    gathered = [
        pltpu.make_async_copy(mine, psi.at[core], psi_sems.at[0]),
        pltpu.make_async_copy(theirs, psi.at[1 - core], psi_sems.at[1]),
    ]
    numbers = [
        pltpu.make_async_copy(in_sector, ins, id_sems.at[0]),
        pltpu.make_async_copy(out_sector, outs, id_sems.at[1]),
        pltpu.make_async_copy(live_terms, lives, id_sems.at[2]),
    ]

    def loads(chunk):
        source = pl.ds(EARLY + chunk * CHUNK, CHUNK)
        part = pl.ds(chunk * CHUNK, CHUNK)
        return [
            pltpu.make_async_copy(left.at[source], lefts.at[part], sems.at[0, chunk]),
            pltpu.make_async_copy(right.at[source], rights.at[part], sems.at[1, chunk]),
        ]

    def wait(chunk, carry):
        for copy in loads(chunk):
            copy.wait()
        return carry

    chunks = (terms - EARLY) // CHUNK
    for copy in numbers:
        copy.start()
    for chunk in range(chunks):
        for copy in loads(chunk):
            copy.start()
    for copy in gathered:
        copy.start()
    total[...] = jnp.zeros_like(total)
    for copy in gathered:
        copy.wait()
    for copy in numbers:
        copy.wait()
    live = lives[0]

    def add(first, shift, lefts, rights):
        for low in range(0, STEP, GROUP):
            middles = []
            for offset in range(low, low + GROUP):
                term = first + offset
                sector = ins[term]
                high = pl.ds((sector >> 2) * 2, 2)
                block = psi[(sector >> 1) & 1, :, high, sector & 1].reshape(256, 256)
                middle = jnp.dot(lefts[term - shift], block, preferred_element_type=jnp.float32)
                middles.append(middle.astype(jnp.bfloat16))
            for offset in range(low, low + GROUP):
                term = first + offset
                out = jnp.where(term < live, outs[term], UNUSED)
                total[out] = total[out] + lax.dot_general(
                    middles[offset - low],
                    rights[term - shift],
                    (((1,), (1,)), ((), ())),
                    preferred_element_type=jnp.float32,
                )

    def early_step(step, carry):
        add(step * STEP, 0, early_left, early_right)
        return carry

    def late_step(step, carry):
        lax.fori_loop(step * (STEP // CHUNK), (step + 1) * (STEP // CHUNK), wait, 0)
        add(EARLY + step * STEP, EARLY, lefts, rights)
        return carry

    used = lax.div(live + STEP - 1, STEP)
    lax.fori_loop(0, jnp.minimum(used, EARLY // STEP), early_step, 0)
    late = jnp.maximum(used - EARLY // STEP, 0)
    lax.fori_loop(0, late, late_step, 0)
    lax.fori_loop(late * (STEP // CHUNK), chunks, wait, 0)
    for high in range(4):
        for low in range(2):
            send[high * 2 + low] = total[4 * high + 2 * (1 - core) + low].astype(jnp.bfloat16)


def product(in_sector, out_sector, live_terms, mine, theirs, early_left, early_right, left, right):
    terms = left.shape[0]
    return pl.pallas_call(
        product_kernel,
        in_specs=[HBM] * 3 + [ANY, ANY, VMEM, VMEM, HBM, HBM],
        out_specs=[VMEM, VMEM],
        scratch_shapes=[
            pltpu.VMEM((2, 16, 8, 2, 8, 256), jnp.bfloat16),
            pltpu.VMEM((terms - EARLY, 256, 256), jnp.bfloat16),
            pltpu.VMEM((terms - EARLY, 256, 256), jnp.bfloat16),
            pltpu.SMEM(in_sector.shape, in_sector.dtype),
            pltpu.SMEM(out_sector.shape, out_sector.dtype),
            pltpu.SMEM(live_terms.shape, live_terms.dtype),
            pltpu.SemaphoreType.DMA((2,)),
            pltpu.SemaphoreType.DMA((3,)),
            pltpu.SemaphoreType.DMA((2, (terms - EARLY) // CHUNK)),
        ],
        out_shape=[
            jax.ShapeDtypeStruct((UNUSED + 1, 256, 256), jnp.float32),
            jax.ShapeDtypeStruct((8, 256, 256), jnp.bfloat16),
        ],
        cost_estimate=pl.CostEstimate(flops=terms * 2**26, transcendentals=0, bytes_accessed=terms * 2**18),
        compiler_params=pltpu.CompilerParams(vmem_limit_bytes=PRODUCT_MIB * 2**20),
    )(in_sector, out_sector, live_terms, mine, theirs, early_left, early_right, left, right)


def merge_kernel(total, other, out):
    core = lax.axis_index("c")
    for pair in range(8):
        sector = 4 * (pair // 2) + 2 * core + pair % 2
        for group in range(32):
            rows = pl.ds(group * 8, 8)
            summed = total[sector, rows, :] + other[pair, rows, :].astype(jnp.float32)
            out[(group % 2) * 16 + group // 2, pair] = summed.astype(jnp.bfloat16)


def merge(total, other):
    return pl.pallas_call(
        merge_kernel,
        in_specs=[VMEM, VMEM],
        out_specs=VMEM,
        out_shape=jax.ShapeDtypeStruct((32, 8, 8, 256), jnp.bfloat16),
        compiler_params=pltpu.CompilerParams(vmem_limit_bytes=6 * 2**20),
    )(total, other)


def local(psi, left_ops, right_ops, in_sector, out_sector, live_terms):
    by_z = spread(psi, ("zh", "zl"), 8)
    mine = spread(by_z, ("y", "x"), 16)
    theirs = swap_cores(mine)
    early_left, early_right = load(left_ops, right_ops)
    total, send = product(
        in_sector, out_sector, live_terms, mine, theirs, early_left, early_right, left_ops, right_ops
    )
    other = swap_cores(send)
    blocks = merge(total, other)
    arrived = lax.all_to_all(blocks, ("zl", "y", "x"), 0, 0)
    rows = arrived.astype(jnp.float32).sum(0)
    last = lax.all_to_all(rows.reshape(4, 2, 8, 256), "zh", 0, 0)
    return last.sum(0)


def solution(mesh):
    torus = Mesh(mesh.devices.reshape(SIZES), AXES)
    op = ("y", "x", "zl")
    sec = ("zh", "c")
    return jax.shard_map(
        local,
        mesh=torus,
        in_specs=(
            P(sec, op, None),
            P(op + sec, None, None),
            P(op + sec, None, None),
            P(op + sec),
            P(op + sec),
            P(op + sec),
        ),
        out_specs=P(sec, op, None),
        check_vma=False,
    )
```

```python
import jax
import jax.numpy as jnp
from jax import lax
from jax.experimental import pallas as pl
from jax.experimental.pallas import tpu as pltpu
from jax.sharding import Mesh, PartitionSpec as P

AXES = ("y", "x", "zl", "zh", "c")
SIZES = (4, 4, 2, 4, 2)
EARLY = 8
CHUNK = 4
LOAD_MIB = 48
PRODUCT_MIB = 40
STEP = 8
GROUP = 4
UNUSED = 16


ANY = pl.BlockSpec(memory_space=pl.ANY)
HBM = pl.BlockSpec(memory_space=pltpu.HBM)
SMEM = pl.BlockSpec(memory_space=pltpu.SMEM)
VMEM = pl.BlockSpec(memory_space=pltpu.VMEM)


def swap_cores(value):
    return lax.ppermute(value, "c", [(0, 1), (1, 0)])


def spread(value, axes, count):
    copies = jnp.broadcast_to(value[None], (count,) + value.shape)
    return lax.all_to_all(copies, axes, 0, 0)


def load_kernel(left, right, lefts, rights, sems):
    copies = []
    for chunk in range(lefts.shape[0] // CHUNK):
        part = pl.ds(chunk * CHUNK, CHUNK)
        copies.append(pltpu.make_async_copy(left.at[part], lefts.at[part], sems.at[0, chunk]))
        copies.append(pltpu.make_async_copy(right.at[part], rights.at[part], sems.at[1, chunk]))
    for copy in copies:
        copy.start()
    for copy in copies:
        copy.wait()


def load(left, right):
    part = jax.ShapeDtypeStruct((EARLY,) + left.shape[1:], left.dtype)
    return pl.pallas_call(
        load_kernel,
        in_specs=[HBM, HBM],
        out_specs=[VMEM, VMEM],
        out_shape=[part, part],
        scratch_shapes=[pltpu.SemaphoreType.DMA((2, EARLY // CHUNK))],
        cost_estimate=pl.CostEstimate(flops=0, transcendentals=0, bytes_accessed=EARLY * 2**18),
        compiler_params=pltpu.CompilerParams(vmem_limit_bytes=LOAD_MIB * 2**20),
    )(left, right)


def product_kernel(
    in_sector, out_sector, live_terms, mine, theirs, early_left, early_right, left, right,
    total, send, psi, lefts, rights, ins, outs, lives, psi_sems, id_sems, sems,
):
    terms = left.shape[0]
    core = lax.axis_index("c")
    gathered = [
        pltpu.make_async_copy(mine, psi.at[core], psi_sems.at[0]),
        pltpu.make_async_copy(theirs, psi.at[1 - core], psi_sems.at[1]),
    ]
    numbers = [
        pltpu.make_async_copy(in_sector, ins, id_sems.at[0]),
        pltpu.make_async_copy(out_sector, outs, id_sems.at[1]),
        pltpu.make_async_copy(live_terms, lives, id_sems.at[2]),
    ]

    def loads(chunk):
        source = pl.ds(EARLY + chunk * CHUNK, CHUNK)
        part = pl.ds(chunk * CHUNK, CHUNK)
        return [
            pltpu.make_async_copy(left.at[source], lefts.at[part], sems.at[0, chunk]),
            pltpu.make_async_copy(right.at[source], rights.at[part], sems.at[1, chunk]),
        ]

    def wait(chunk, carry):
        for copy in loads(chunk):
            copy.wait()
        return carry

    chunks = (terms - EARLY) // CHUNK
    for copy in numbers:
        copy.start()
    for chunk in range(chunks):
        for copy in loads(chunk):
            copy.start()
    for copy in gathered:
        copy.start()
    total[...] = jnp.zeros_like(total)
    for copy in gathered:
        copy.wait()
    for copy in numbers:
        copy.wait()
    live = lives[0]

    def add(first, shift, lefts, rights, width=STEP):
        for low in range(0, width, GROUP):
            middles = []
            for offset in range(low, low + GROUP):
                term = first + offset
                sector = ins[term]
                high = pl.ds((sector >> 2) * 2, 2)
                block = psi[(sector >> 1) & 1, :, high, sector & 1].reshape(256, 256)
                middle = jnp.dot(lefts[term - shift], block, preferred_element_type=jnp.float32)
                middles.append(middle.astype(jnp.bfloat16))
            for offset in range(low, low + GROUP):
                term = first + offset
                out = jnp.where(term < live, outs[term], UNUSED)
                total[out] = total[out] + lax.dot_general(
                    middles[offset - low],
                    rights[term - shift],
                    (((1,), (1,)), ((), ())),
                    preferred_element_type=jnp.float32,
                )

    def early_step(step, carry):
        add(step * STEP, 0, early_left, early_right)
        return carry

    def late_step(step, carry):
        lax.fori_loop(step * (STEP // CHUNK), (step + 1) * (STEP // CHUNK), wait, 0)
        add(EARLY + step * STEP, EARLY, lefts, rights)
        return carry

    used = lax.div(live + STEP - 1, STEP)
    lax.fori_loop(0, jnp.minimum(used, EARLY // STEP), early_step, 0)
    late = jnp.maximum(used - EARLY // STEP, 0)
    lax.fori_loop(0, late - 1, late_step, 0)

    def last_step(chunk, carry):
        wait(chunk, carry)
        add(EARLY + chunk * CHUNK, EARLY, lefts, rights, CHUNK)
        return carry

    per_step = STEP // CHUNK
    lax.fori_loop(jnp.maximum(late - 1, 0) * per_step, late * per_step, last_step, 0)
    lax.fori_loop(late * (STEP // CHUNK), chunks, wait, 0)
    for high in range(4):
        for low in range(2):
            send[high * 2 + low] = total[4 * high + 2 * (1 - core) + low].astype(jnp.bfloat16)


def product(in_sector, out_sector, live_terms, mine, theirs, early_left, early_right, left, right):
    terms = left.shape[0]
    return pl.pallas_call(
        product_kernel,
        in_specs=[HBM] * 3 + [ANY, ANY, VMEM, VMEM, HBM, HBM],
        out_specs=[VMEM, VMEM],
        scratch_shapes=[
            pltpu.VMEM((2, 16, 8, 2, 8, 256), jnp.bfloat16),
            pltpu.VMEM((terms - EARLY, 256, 256), jnp.bfloat16),
            pltpu.VMEM((terms - EARLY, 256, 256), jnp.bfloat16),
            pltpu.SMEM(in_sector.shape, in_sector.dtype),
            pltpu.SMEM(out_sector.shape, out_sector.dtype),
            pltpu.SMEM(live_terms.shape, live_terms.dtype),
            pltpu.SemaphoreType.DMA((2,)),
            pltpu.SemaphoreType.DMA((3,)),
            pltpu.SemaphoreType.DMA((2, (terms - EARLY) // CHUNK)),
        ],
        out_shape=[
            jax.ShapeDtypeStruct((UNUSED + 1, 256, 256), jnp.float32),
            jax.ShapeDtypeStruct((8, 256, 256), jnp.bfloat16),
        ],
        cost_estimate=pl.CostEstimate(flops=terms * 2**26, transcendentals=0, bytes_accessed=terms * 2**18),
        compiler_params=pltpu.CompilerParams(vmem_limit_bytes=PRODUCT_MIB * 2**20),
    )(in_sector, out_sector, live_terms, mine, theirs, early_left, early_right, left, right)


def merge_kernel(total, other, out):
    core = lax.axis_index("c")
    for pair in range(8):
        sector = 4 * (pair // 2) + 2 * core + pair % 2
        for group in range(32):
            rows = pl.ds(group * 8, 8)
            summed = total[sector, rows, :] + other[pair, rows, :].astype(jnp.float32)
            out[(group % 2) * 16 + group // 2, pair] = summed.astype(jnp.bfloat16)


def merge(total, other):
    return pl.pallas_call(
        merge_kernel,
        in_specs=[VMEM, VMEM],
        out_specs=VMEM,
        out_shape=jax.ShapeDtypeStruct((32, 8, 8, 256), jnp.bfloat16),
        compiler_params=pltpu.CompilerParams(vmem_limit_bytes=6 * 2**20),
    )(total, other)


def local(psi, left_ops, right_ops, in_sector, out_sector, live_terms):
    by_z = spread(psi, ("zh", "zl"), 8)
    mine = spread(by_z, ("y", "x"), 16)
    theirs = swap_cores(mine)
    early_left, early_right = load(left_ops, right_ops)
    total, send = product(
        in_sector, out_sector, live_terms, mine, theirs, early_left, early_right, left_ops, right_ops
    )
    other = swap_cores(send)
    blocks = merge(total, other)
    arrived = lax.all_to_all(blocks, ("zl", "y", "x"), 0, 0)
    rows = arrived.astype(jnp.float32).sum(0)
    last = lax.all_to_all(rows.reshape(4, 2, 8, 256), "zh", 0, 0)
    return last.sum(0)


def solution(mesh):
    torus = Mesh(mesh.devices.reshape(SIZES), AXES)
    op = ("y", "x", "zl")
    sec = ("zh", "c")
    return jax.shard_map(
        local,
        mesh=torus,
        in_specs=(
            P(sec, op, None),
            P(op + sec, None, None),
            P(op + sec, None, None),
            P(op + sec),
            P(op + sec),
            P(op + sec),
        ),
        out_specs=P(sec, op, None),
        check_vma=False,
    )
```
